256 devices in a mesh: member: 16 (over x, y_hi, core), tile: 16 (over z, y_lo).
Axes of the slice: x: 4, y: 4 (y_hi: 2, y_lo: 2; y = y_hi * 2 + y_lo), z: 8, core: 2. Of those that a mesh axis runs over, the one named last changes fastest.
Arguments:
- control: float32 [256, 16, 4, 4096], P('member', 'tile'), may hold values from -6 to 6
- perturbations: float32 [256, 16, 4, 4, 4096], P('member', 'tile'), may hold values from -1.5 to 1.5
- diffusivity: float32 [16, 4096], P('tile'), may hold values from 0.02 to 0.24
- flow: float32 [2, 16, 4, 4], P(None, 'tile'), may hold values from 0.02 to 0.22
- observed: float32 [16, 4, 4, 4096], P('tile'), may hold values from -6 to 6
- obs_weight: float32 [16, 4, 4, 4096], P('tile'), may hold values from 0.3 to 3
- neighbour_tile: int32 [16, 4], replicated, may hold values from 0 to 15, as said below
- neighbour_edge: int32 [16, 4], replicated, may hold values from 0 to 3
- departure: int32 [16, 4, 64], replicated, may hold values from 0 to 63, as said below
Outputs:
- gradient: float32 [256, 16, 4, 4096], P('member', 'tile')
The draws below stay inside these ranges and needn't reach their ends.
Inputs may be any that keep to these rules, and one draw needn't show every extreme that they name: `neighbour_tile`: edges are glued in pairs: if edge e of tile t meets edge e2 of tile u, then edge e2 of tile u meets edge e of tile t. `departure`: each row is 0 to 63 in order or reversed, the same way for both edges of a glued pair.
All inputs are finite; a program needn't handle non-finite values.
Results may differ from the reference program's by a relative error of at most 0.0001.
Values sent between devices are 32-bit elements; how exact they have to be, the bound alone decides.
No kernel may reach another device: no remote copies, remote signals or barrier semaphores. Data moves between devices by JAX's collectives and lax.ppermute only.
A program may use at most 128 MiB of HBM per device.

```python
import math
import jax
import jax.numpy as jnp
from jax import lax

S = 64
V = 4
L = 4
SWEEPS = 8
STEPS = 2
MEMBERS = 256
TILES = 16
CELLS = 4096


def glued_edges(key):
    slot_count = 4 * TILES
    shuffled = jax.random.permutation(jax.random.fold_in(key, 101), slot_count).astype(jnp.int32)
    firsts = shuffled[0::2]
    seconds = shuffled[1::2]
    partner = jnp.zeros((slot_count,), jnp.int32).at[firsts].set(seconds).at[seconds].set(firsts)
    flip_bits = jax.random.randint(jax.random.fold_in(key, 202), (slot_count // 2,), 0, 2).astype(jnp.int32)
    flipped = jnp.zeros((slot_count,), jnp.int32).at[firsts].set(flip_bits).at[seconds].set(flip_bits)
    return (partner, flipped)


def draw_neighbour_tile(key, part):
    partner, flipped = glued_edges(key)
    return (partner // 4).reshape(TILES, 4)


def draw_neighbour_edge(key, part):
    partner, flipped = glued_edges(key)
    return (partner % 4).reshape(TILES, 4)


def draw_departure(key, part):
    partner, flipped = glued_edges(key)
    positions = jnp.arange(S, dtype=jnp.int32)
    indices = jnp.where(flipped[:, None] == 1, S - 1 - positions[None, :], positions[None, :])
    return indices.reshape(TILES, 4, S).astype(jnp.int32)


def block_levels(own_key, shape, pieces, low, largest):
    gain = 1.0
    for position, blocks in pieces:
        draws = jax.random.uniform(jax.random.fold_in(jax.random.fold_in(own_key, 6), position), (blocks,), jnp.float32, low / len(pieces), largest / len(pieces))
        gain = gain * jnp.repeat(jnp.exp(draws), shape[position] // blocks).reshape((-1,) + (1,) * (len(shape) - 1 - position))
    return gain


def noise(key, shape, spread, most, pieces=(), kind=jnp.bfloat16):
    array = spread * jax.random.normal(key, shape, jnp.float32)
    if pieces:
        array = array * block_levels(key, shape, pieces, -0.22, 0.18)
    return jnp.clip(array, -most, most).astype(kind)


def setup_inputs(seed: int = 0) -> dict:
    streams_of = jax.random.split(jax.random.key(seed), 10)
    return {
        "control": noise(streams_of[0], (MEMBERS, TILES, L, CELLS), 1.0, 6.0, ((0, 16), (1, 16)), jnp.float32),
        "perturbations": noise(streams_of[1], (MEMBERS, TILES, V, L, CELLS), (MEMBERS // 16) ** -0.5, 1.5, ((0, 16), (1, 16)), jnp.float32),
        "diffusivity": jnp.clip(jnp.exp(math.log(0.24) - 2.4849066 * jax.random.uniform(streams_of[2], (TILES, CELLS), jnp.float32) ** block_levels(streams_of[2], (TILES, CELLS), ((0, 16),), -0.2, 0.2)), 0.02, 0.24),
        "flow": jnp.clip(0.02 + 0.2 * jax.random.uniform(streams_of[3], (STEPS, TILES, L, 4), jnp.float32) ** block_levels(streams_of[3], (STEPS, TILES, L, 4), ((1, 16),), -0.2, 0.2), 0.02, 0.22),
        "observed": noise(streams_of[4], (TILES, V, L, CELLS), 1.0, 6.0, ((0, 16),), jnp.float32),
        "obs_weight": jnp.clip(jnp.exp(math.log(3.0) - 2.3025851 * jax.random.uniform(streams_of[5], (TILES, V, L, CELLS), jnp.float32) ** block_levels(streams_of[5], (TILES, V, L, CELLS), ((0, 16),), -0.2, 0.2)), 0.3, 3.0),
        "neighbour_tile": draw_neighbour_tile(jax.random.fold_in(streams_of[9], 71), 0),
        "neighbour_edge": draw_neighbour_edge(jax.random.fold_in(streams_of[9], 71), 0),
        "departure": draw_departure(jax.random.fold_in(streams_of[9], 71), 0),
    }


PRECISE = lax.Precision.HIGHEST


def edge_strips(values):
    return jnp.stack([values[..., 0, :], values[..., -1, :], values[..., :, 0], values[..., :, -1]], axis=2)


def combine(values, ghosts, factors):
    before_rows = jnp.concatenate([ghosts[:, :, 0, :, None, :], values[..., :-1, :]], axis=-2)
    after_rows = jnp.concatenate([values[..., 1:, :], ghosts[:, :, 1, :, None, :]], axis=-2)
    before_cols = jnp.concatenate([ghosts[:, :, 2, :, :, None], values[..., :, :-1]], axis=-1)
    after_cols = jnp.concatenate([values[..., :, 1:], ghosts[:, :, 3, :, :, None]], axis=-1)
    return (factors[0] * values + factors[1] * before_rows + factors[2] * after_rows
            + factors[3] * before_cols + factors[4] * after_cols)


def spread_back(values, factors):
    parts = [factors[1 + which] * values for which in range(4)]
    zero_row = jnp.zeros_like(values[..., :1, :])
    zero_col = jnp.zeros_like(values[..., :, :1])
    inner = factors[0] * values
    inner = inner + jnp.concatenate([parts[0][..., 1:, :], zero_row], axis=-2)
    inner = inner + jnp.concatenate([zero_row, parts[1][..., :-1, :]], axis=-2)
    inner = inner + jnp.concatenate([parts[2][..., :, 1:], zero_col], axis=-1)
    inner = inner + jnp.concatenate([zero_col, parts[3][..., :, :-1]], axis=-1)
    outward = jnp.stack([parts[0][..., 0, :], parts[1][..., -1, :], parts[2][..., :, 0], parts[3][..., :, -1]], axis=2)
    return inner, outward


def add_edges(inner, incoming):
    zero_rows = jnp.zeros_like(inner[..., 1:, :])
    zero_cols = jnp.zeros_like(inner[..., :, 1:])
    inner = inner + jnp.concatenate([incoming[:, :, 0, :, None, :], zero_rows], axis=-2)
    inner = inner + jnp.concatenate([zero_rows, incoming[:, :, 1, :, None, :]], axis=-2)
    inner = inner + jnp.concatenate([incoming[:, :, 2, :, :, None], zero_cols], axis=-1)
    inner = inner + jnp.concatenate([zero_cols, incoming[:, :, 3, :, :, None]], axis=-1)
    return inner


def forward_map(values, factors, tables):
    neighbour_tile, neighbour_edge, permute = tables
    strips = edge_strips(values)
    picked = strips[:, neighbour_tile, neighbour_edge]
    ghosts = jnp.einsum("pteqm,tekm->pteqk", picked, permute, precision=PRECISE)
    return combine(values, ghosts, factors)


def adjoint_map(values, factors, tables):
    neighbour_tile, neighbour_edge, permute = tables
    inner, outward = spread_back(values, factors)
    sent = jnp.einsum("pteqk,tekm->pteqm", outward, permute, precision=PRECISE)
    incoming = jnp.zeros_like(sent).at[:, neighbour_tile, neighbour_edge].add(sent)
    return add_edges(inner, incoming)


def reference(control, perturbations, diffusivity, flow, observed, obs_weight, neighbour_tile, neighbour_edge, departure):
    permute = (departure[..., None] == jnp.arange(S, dtype=jnp.int32)).astype(jnp.float32)
    tables = (neighbour_tile, neighbour_edge, permute)
    rate = diffusivity.reshape(1, TILES, 1, S, S)
    smooth_factors = (1.0 - 4.0 * rate, rate, rate, rate, rate)

    def smooth(values, adjoint):
        grid = values.reshape(1, TILES, L, S, S)
        for repeat in range(SWEEPS):
            if adjoint:
                grid = adjoint_map(grid, smooth_factors, tables)
            else:
                grid = forward_map(grid, smooth_factors, tables)
        return grid[0]

    def accumulate(running, member_pair):
        member_control, member_pert = member_pair
        smoothed = smooth(member_control, False)
        return running + member_pert.reshape(TILES, V, L, S, S) * smoothed[:, None], None

    increment = lax.scan(accumulate, jnp.zeros((TILES, V, L, S, S), jnp.float32), (control, perturbations))[0]

    def flow_factors(section):
        speeds = jnp.tile(flow[section], (1, V, 1))[None, :, :, :, None, None]
        return (1.0 - jnp.sum(speeds, axis=3), speeds[:, :, :, 0], speeds[:, :, :, 1],
                speeds[:, :, :, 2], speeds[:, :, :, 3])

    state = increment.reshape(1, TILES, V * L, S, S)
    for section in range(STEPS):
        state = forward_map(state, flow_factors(section), tables)
    misfit = obs_weight.reshape(1, TILES, V * L, S, S) * (state - observed.reshape(1, TILES, V * L, S, S))
    for section in reversed(range(STEPS)):
        misfit = adjoint_map(misfit, flow_factors(section), tables)
    sensitivity = misfit.reshape(TILES, V, L, S * S)

    def gradient_of(member_pair):
        member_control, member_pert = member_pair
        projected = jnp.sum(member_pert * sensitivity, axis=1)
        return member_control + smooth(projected, True).reshape(TILES, L, S * S)

    return lax.map(gradient_of, (control, perturbations))
```

```python
import functools

import jax
import jax.numpy as jnp
from jax import lax
from jax.experimental import pallas as pl
from jax.experimental.pallas import tpu as pltpu
from jax.sharding import PartitionSpec as P

S = 64
V = 4
L = 4
SWEEPS = 8
STEPS = 2
TILES = 16
PAIRS = TILES // 2
ROWS = 32
FIELD = L * ROWS
EXTRA = 3 * ROWS + 8
f32 = jnp.float32


def iota(axis):
    return lax.broadcasted_iota(jnp.int32, (8, 128), axis)


def turn(x, shift):
    shift %= 128
    return pltpu.roll(x, shift, 1) if shift else x


def swap(x):
    return pltpu.roll(x, 4, 0)


def pick(x, index):
    return jnp.take_along_axis(x, index, axis=1, mode="promise_in_bounds")


def split_halves(cells):
    low = iota(1) < S
    out = []
    for c in range(ROWS // 2):
        first, second = cells[c], cells[c + ROWS // 2]
        out.append(jnp.where(low, first, turn(second, S)))
        out.append(jnp.where(low, turn(first, S), second))
    return out


def join_halves(rows):
    low = iota(1) < S
    out = [None] * ROWS
    for c in range(ROWS // 2):
        even, odd = rows[2 * c], rows[2 * c + 1]
        out[c] = jnp.where(low, even, turn(odd, S))
        out[c + ROWS // 2] = jnp.where(low, turn(even, S), odd)
    return out


def edge_mask():
    column = iota(1) % S
    return (column == 0) | (column == S - 1)


def column_sum(values):
    mask = edge_mask()
    parts = [turn(jnp.where(mask, values[r], 0.0), 2 * r) for r in range(ROWS)]
    while len(parts) > 1:
        parts = [a + b for a, b in zip(parts[0::2], parts[1::2])]
    return parts[0]


def strips_of(top, bottom, columns):
    lane = iota(1)
    place = jnp.where(lane < S, lane, 127 - lane)
    return (
        pick(top, place),
        pick(bottom, place + S),
        pick(columns, 2 * place),
        pick(columns, (2 * place + 63) % 128),
    )


def placed_ghosts(ghosts, flips):
    lane = iota(1)
    even = lane % 2 == 0
    along = lane % S
    top = pick(ghosts[0], along + flips[0])
    bottom = pick(ghosts[1], along + flips[1])
    left = pick(ghosts[2], lane // 2 + flips[2])
    right = pick(ghosts[3], ((lane + 65) % 128) // 2 + flips[3])
    return top, bottom, jnp.where(even, left, right)


def smooth_kernel(adjoint, src_ref, flag_ref, x_ref, *refs):
    if adjoint:
        rate_ref, out_ref, state_ref, field_ref, strip_ref = refs
    else:
        out_ref, rate_ref, target_ref, speed_ref, field_ref, strip_ref = refs
    lower = iota(0) < 4
    low = iota(1) < S
    column = iota(1) % S

    def save_strips(slot, pair, top, bottom, columns):
        for edge, strip in enumerate(strips_of(top, bottom, columns)):
            strip_ref[slot, edge * TILES + 2 * pair] = strip
            strip_ref[slot, edge * TILES + 2 * pair + 1] = swap(strip)

    def load(pair, carry):
        cells = [None] * ROWS
        for k in range(ROWS // 2):
            a = x_ref[2 * pair, pl.ds(8 * k, 8), :]
            b = x_ref[2 * pair + 1, pl.ds(8 * k, 8), :]
            cells[2 * k] = jnp.where(lower, a, swap(b))
            cells[2 * k + 1] = jnp.where(lower, swap(a), b)
        values = split_halves(cells)
        if not adjoint:
            rates = []
            for c in range(ROWS):
                a = x_ref[2 * pair, pl.ds(FIELD + c, 1), :]
                b = x_ref[2 * pair + 1, pl.ds(FIELD + c, 1), :]
                rates.append(
                    jnp.where(lower, jnp.broadcast_to(a, (8, 128)), jnp.broadcast_to(b, (8, 128)))
                )
            rates = split_halves(rates)
            for r in range(ROWS):
                rate_ref[pair, r] = rates[r]
        if adjoint:
            for r in range(ROWS):
                state_ref[pair, r] = values[r]
            values = [values[r] * rate_ref[pair, r] for r in range(ROWS)]
        for r in range(ROWS):
            field_ref[pair, r] = values[r]
        save_strips(0, pair, values[0], values[ROWS - 1], column_sum(values))
        return carry

    lax.fori_loop(0, PAIRS, load, 0)

    def sweep(repeat, carry):
        slot = repeat % 2

        def one(pair, carry):
            ghosts, flips = [], []
            for d in range(4):
                first = strip_ref[slot, src_ref[8 * pair + d]]
                second = strip_ref[slot, src_ref[8 * pair + 4 + d] ^ 1]
                ghosts.append(jnp.where(lower, first, second))
                flips.append(jnp.where(lower, flag_ref[8 * pair + d], flag_ref[8 * pair + 4 + d]))
            top, bottom, sides = placed_ghosts(ghosts, flips)
            first = field_ref[pair, 0]
            last = field_ref[pair, ROWS - 1]
            before = jnp.where(low, top, turn(last, S))
            wrapped = jnp.where(low, turn(first, S), bottom)
            here = first
            mask = edge_mask()
            columns = None
            new_first = new_last = None
            for r in range(ROWS):
                after = field_ref[pair, r + 1] if r < ROWS - 1 else wrapped
                side = turn(sides, -2 * r)
                left = jnp.where(column == 0, side, turn(here, 1))
                right = jnp.where(column == S - 1, side, turn(here, -1))
                change = (before + after) + (left + right) - 4.0 * here
                if adjoint:
                    state = state_ref[pair, r] + change
                    state_ref[pair, r] = state
                    new = state * rate_ref[pair, r]
                else:
                    new = here + rate_ref[pair, r] * change
                field_ref[pair, r] = new
                edge = turn(jnp.where(mask, new, 0.0), 2 * r)
                columns = edge if columns is None else columns + edge
                if r == 0:
                    new_first = new
                new_last = new
                before, here = here, after
            save_strips(1 - slot, pair, new_first, new_last, columns)
            return carry

        lax.fori_loop(0, PAIRS, one, 0)
        return carry

    lax.fori_loop(0, SWEEPS, sweep, 0)

    result_ref = state_ref if adjoint else field_ref

    def store(pair, carry):
        cells = join_halves([result_ref[pair, r] for r in range(ROWS)])
        for k in range(ROWS // 2):
            a, b = cells[2 * k], cells[2 * k + 1]
            out_ref[2 * pair, pl.ds(8 * k, 8), :] = jnp.where(lower, a, swap(b))
            out_ref[2 * pair + 1, pl.ds(8 * k, 8), :] = jnp.where(lower, swap(a), b)
        return carry

    lax.fori_loop(0, PAIRS, store, 0)

    if not adjoint:
        for group in range(2):
            tiles = pl.ds(8 * group, 8)
            for kind in range(2):
                start = FIELD + ROWS + kind * ROWS
                cells = split_halves([x_ref[tiles, start + c, :] for c in range(ROWS)])
                for r in range(ROWS):
                    target_ref[kind, group, r] = cells[r]
            speeds = x_ref[tiles, FIELD + 3 * ROWS, :]
            for k in range(4 * STEPS):
                speed_ref[group, k] = jnp.broadcast_to(speeds[:, k : k + 1], (8, 128))


VMEM = pl.BlockSpec(memory_space=pltpu.VMEM)
SMEM = pl.BlockSpec(memory_space=pltpu.SMEM)
BOUND = 56 * 1024 * 1024


def shape(*dims):
    return jax.ShapeDtypeStruct(dims, f32)


def smooth_forward(src, flag, received):
    return pl.pallas_call(
        functools.partial(smooth_kernel, False),
        out_shape=(
            shape(TILES, FIELD, 128),
            shape(PAIRS, ROWS, 8, 128),
            shape(2, 2, ROWS, 8, 128),
            shape(2, 4 * STEPS, 8, 128),
        ),
        in_specs=[SMEM, SMEM, VMEM],
        out_specs=(VMEM, VMEM, VMEM, VMEM),
        scratch_shapes=[
            pltpu.VMEM((PAIRS, ROWS, 8, 128), f32),
            pltpu.VMEM((2, 4 * TILES, 8, 128), f32),
        ],
        name="smooth_forward",
    )(src, flag, received)


def smooth_adjoint(src, flag, received, rate):
    return pl.pallas_call(
        functools.partial(smooth_kernel, True),
        out_shape=shape(TILES, FIELD, 128),
        in_specs=[SMEM, SMEM, VMEM, VMEM],
        out_specs=VMEM,
        scratch_shapes=[
            pltpu.VMEM((PAIRS, ROWS, 8, 128), f32),
            pltpu.VMEM((PAIRS, ROWS, 8, 128), f32),
            pltpu.VMEM((2, 4 * TILES, 8, 128), f32),
        ],
        name="smooth_adjoint",
    )(src, flag, received, rate)


def transport_kernel(
    src_ref, own_ref, flip_ref, x_ref, target_ref, speed_ref, out_ref, field_ref, strip_ref, ghost_ref, plain_ref
):
    low = iota(1) < S
    column = iota(1) % S
    mask = edge_mask()

    def save_strips(group, strips):
        for edge in range(4):
            strip_ref[pl.ds(edge * TILES + 8 * group, 8), :] = strips[edge]

    def fetch():
        for tile in range(TILES):
            for d in range(4):
                ghost_ref[pl.ds(d * TILES + tile, 1), :] = strip_ref[pl.ds(src_ref[4 * tile + d], 1), :]

    def step(section, adjoint):
        for group in range(2):
            values = [field_ref[group, r] for r in range(ROWS)]
            strips = strips_of(values[0], values[-1], column_sum(values))
            if adjoint:
                strips = [strips[d] * speed_ref[group, 4 * section + d] for d in range(4)]
            save_strips(group, strips)
        fetch()
        for group in range(2):
            c = [speed_ref[group, 4 * section + d] for d in range(4)]
            keep = 1.0 - ((c[0] + c[1]) + (c[2] + c[3]))
            tiles = [pl.ds(d * TILES + 8 * group, 8) for d in range(4)]
            ghosts = [ghost_ref[tiles[d], :] for d in range(4)]
            if not adjoint:
                ghosts = [ghosts[d] * c[d] for d in range(4)]
            else:
                c = [c[1], c[0], c[3], c[2]]
            flips = [flip_ref[tiles[d], :] for d in range(4)]
            top, bottom, sides = placed_ghosts(ghosts, flips)
            first = field_ref[group, 0]
            last = field_ref[group, ROWS - 1]
            previous = None
            here = first
            for r in range(ROWS):
                after = field_ref[group, r + 1] if r < ROWS - 1 else None
                side = turn(sides, -2 * r)
                left = jnp.where(column == 0, side, c[2] * turn(here, 1))
                right = jnp.where(column == S - 1, side, c[3] * turn(here, -1))
                if r == 0:
                    up = jnp.where(low, top, c[0] * turn(last, S))
                else:
                    up = c[0] * previous
                if r == ROWS - 1:
                    down = jnp.where(low, c[1] * turn(first, S), bottom)
                else:
                    down = c[1] * after
                new = keep * here + (up + down) + (left + right)
                if section == STEPS - 1 and not adjoint:
                    new = target_ref[0, group, r] * (new - target_ref[1, group, r])
                field_ref[group, r] = new
                previous, here = here, after

    for group in range(2):
        rows = split_halves([x_ref[pl.ds(8 * group, 8), c, :] for c in range(ROWS)])
        for r in range(ROWS):
            field_ref[group, r] = rows[r]
    for section in range(STEPS):
        step(section, False)
    for section in reversed(range(STEPS)):
        step(section, True)
    for group in range(2):
        cells = join_halves([field_ref[group, r] for r in range(ROWS)])
        for c in range(ROWS):
            plain_ref[pl.ds(8 * group, 8), c, :] = cells[c]
    mine = plain_ref[own_ref[0]]
    for other in range(out_ref.shape[0]):
        out_ref[other] = mine


def transport(src, own, flip, gathered, target, speed, copies):
    return pl.pallas_call(
        transport_kernel,
        out_shape=shape(copies, ROWS, 128),
        in_specs=[SMEM, SMEM, VMEM, VMEM, VMEM, VMEM],
        out_specs=VMEM,
        scratch_shapes=[
            pltpu.VMEM((2, ROWS, 8, 128), f32),
            pltpu.VMEM((4 * TILES, 128), f32),
            pltpu.VMEM((4 * TILES, 128), f32),
            pltpu.VMEM((TILES, ROWS, 128), f32),
        ],
        name="transport",
    )(src, own, flip, gathered, target, speed)


def exchange(values, axis):
    return lax.all_to_all(values, axis, split_axis=0, concat_axis=0, tiled=True)


def to_lines(fields):
    lead = fields.shape[:-2]
    fields = fields.reshape(*lead, L, ROWS, 128)
    return jnp.swapaxes(fields, -3, -2).reshape(*lead, FIELD, 128)


def from_lines(lines):
    lead = lines.shape[:-2]
    lines = lines.reshape(*lead, ROWS, L, 128)
    return jnp.swapaxes(lines, -3, -2).reshape(*lead, L, ROWS * 128)


def body(
    control,
    perturbations,
    diffusivity,
    flow,
    observed,
    obs_weight,
    neighbour_tile,
    neighbour_edge,
    departure,
):
    source = (neighbour_edge * TILES + neighbour_tile).reshape(-1)
    flips = (departure[:, :, 0] != 0).astype(jnp.int32) * S
    flag = flips.reshape(-1)
    flip = jnp.broadcast_to(flips.T.reshape(4 * TILES, 1), (4 * TILES, 128))
    own = lax.axis_index("tile").reshape(1)
    row = lax.axis_index("member")
    members = control.shape[0]

    control_lines = to_lines(control[:, 0])
    weight = lax.dynamic_slice_in_dim(obs_weight.reshape(V * L, ROWS * 128), row, 1, 0)
    target = lax.dynamic_slice_in_dim(observed.reshape(V * L, ROWS * 128), row, 1, 0)
    speeds = lax.dynamic_slice_in_dim(flow[:, 0], row % L, 1, 1).reshape(1, STEPS * 4)
    extra = jnp.concatenate(
        [
            diffusivity.reshape(ROWS, 128),
            weight.reshape(ROWS, 128),
            target.reshape(ROWS, 128),
            jnp.pad(speeds, ((0, 7), (0, 128 - STEPS * 4))),
        ],
        axis=0,
    )
    sent = jnp.concatenate(
        [control_lines, jnp.broadcast_to(extra[None], (members, EXTRA, 128))], axis=1
    )
    smoothed, rate, goal, speed = smooth_forward(source, flag, exchange(sent, "tile"))
    smoothed = exchange(smoothed, "tile")

    spread = to_lines(perturbations[:, 0])
    partial = jnp.sum(spread * smoothed[:, None], axis=0)
    partial = jnp.swapaxes(partial.reshape(V, ROWS, L, 128), 1, 2).reshape(V * L, ROWS, 128)
    increment = jnp.sum(exchange(partial, "member"), axis=0)
    gathered = exchange(jnp.broadcast_to(increment[None], (TILES, ROWS, 128)), "tile")
    sensitivity = exchange(transport(source, own, flip, gathered, goal, speed, V * L), "member")
    sensitivity = jnp.swapaxes(sensitivity.reshape(V, L, ROWS, 128), 1, 2).reshape(V, FIELD, 128)

    projected = jnp.sum(spread * sensitivity[None], axis=1)
    mixed = exchange(smooth_adjoint(source, flag, exchange(projected, "tile"), rate), "tile")
    return control + from_lines(mixed)[:, None]


def solution(mesh):
    in_specs = (
        P("member", "tile", None, None),
        P("member", "tile", None, None, None),
        P("tile", None),
        P(None, "tile", None, None),
        P("tile", None, None, None),
        P("tile", None, None, None),
        P(),
        P(),
        P(),
    )
    out_specs = P("member", "tile", None, None)
    return jax.shard_map(body, mesh=mesh, in_specs=in_specs, out_specs=out_specs, check_vma=False)
```

```python
import functools

import jax
import jax.numpy as jnp
from jax import lax
from jax.experimental import pallas as pl
from jax.experimental.pallas import tpu as pltpu
from jax.sharding import PartitionSpec as P

S = 64
V = 4
L = 4
SWEEPS = 8
STEPS = 2
TILES = 16
PAIRS = TILES // 2
ROWS = 32
FIELD = L * ROWS
LINES = 14
FRAME = L * LINES
SERIES = 8 * SWEEPS
EXTRA = 48
f32 = jnp.float32


def iota(axis):
    return lax.broadcasted_iota(jnp.int32, (8, 128), axis)


def turn(x, shift):
    shift %= 128
    return pltpu.roll(x, shift, 1) if shift else x


def swap(x):
    return pltpu.roll(x, 4, 0)


def pick(x, index):
    return jnp.take_along_axis(x, index, axis=1, mode="promise_in_bounds")


def split_halves(cells):
    low = iota(1) < S
    out = []
    for c in range(ROWS // 2):
        first, second = cells[c], cells[c + ROWS // 2]
        out.append(jnp.where(low, first, turn(second, S)))
        out.append(jnp.where(low, turn(first, S), second))
    return out


def join_halves(rows):
    low = iota(1) < S
    out = [None] * ROWS
    for c in range(ROWS // 2):
        even, odd = rows[2 * c], rows[2 * c + 1]
        out[c] = jnp.where(low, even, turn(odd, S))
        out[c + ROWS // 2] = jnp.where(low, turn(even, S), odd)
    return out


def edge_mask():
    column = iota(1) % S
    return (column == 0) | (column == S - 1)


def column_sum(values):
    mask = edge_mask()
    parts = [turn(jnp.where(mask, values[r], 0.0), 2 * r) for r in range(ROWS)]
    while len(parts) > 1:
        parts = [a + b for a, b in zip(parts[0::2], parts[1::2])]
    return parts[0]


def strips_of(top, bottom, columns):
    lane = iota(1)
    place = jnp.where(lane < S, lane, 127 - lane)
    return (
        pick(top, place),
        pick(bottom, place + S),
        pick(columns, 2 * place),
        pick(columns, (2 * place + 63) % 128),
    )


def placed_ghosts(ghosts, flips):
    lane = iota(1)
    even = lane % 2 == 0
    along = lane % S
    top = pick(ghosts[0], along + flips[0])
    bottom = pick(ghosts[1], along + flips[1])
    left = pick(ghosts[2], lane // 2 + flips[2])
    right = pick(ghosts[3], ((lane + 65) % 128) // 2 + flips[3])
    return top, bottom, jnp.where(even, left, right)


def line_of(c):
    if c < 4:
        return c, 0
    if c >= ROWS - 4:
        return c - (ROWS - 8), 0
    block = c // 2 - 2
    return 8 + 2 * (block // 4) + c % 2, 16 * (block % 4)


def unpack(lines):
    return [turn(lines[line_of(c)[0]], -line_of(c)[1]) for c in range(ROWS)]


def gather_blocks(cells):
    lane = iota(1)
    packed = cells[0]
    for j in range(1, 4):
        packed = jnp.where((lane + 8 - 16 * j) % S < 16, turn(cells[j], 16 * j), packed)
    return packed


def pair_cells(a, b):
    lower = iota(0) < 4
    cells = []
    for x, y in zip(a, b):
        cells.append(jnp.where(lower, x, swap(y)))
        cells.append(jnp.where(lower, swap(x), y))
    return cells


def spread_row(row):
    return jnp.broadcast_to(row, (8, 128))


def pack_kernel(*refs):
    x_ref, *refs = refs
    out_ref = refs[-3] if len(refs) > 1 else refs[-1]

    def one(member, carry):
        cells = [x_ref[member, pl.ds(8 * k, 8), :] for k in range(ROWS // 2)]
        for place, k in enumerate((0, 1, 14, 15)):
            out_ref[member, pl.ds(8 * place, 8), :] = cells[k]
        for g in range(3):
            out_ref[member, pl.ds(32 + 8 * g, 8), :] = gather_blocks(cells[2 + 4 * g : 6 + 4 * g])
        return carry

    members = x_ref.shape[0]
    lax.fori_loop(0, members, one, 0, unroll=4)
    if len(refs) > 1:
        own_ref, flow_ref, rate_ref, weight_ref, target_ref, out_ref, rows_ref, pack_ref = refs
        variable, level = own_ref[0], own_ref[1]
        for c in range(ROWS):
            line = pl.ds(L * c + level, 1)
            rows_ref[0, pl.ds(c, 1), :] = rate_ref[pl.ds(c, 1), :]
            rows_ref[1, pl.ds(c, 1), :] = weight_ref[variable, line, :]
            rows_ref[2, pl.ds(c, 1), :] = target_ref[variable, line, :]
        for kind in range(3):
            base = kind * LINES
            for place, c in enumerate((0, 1, 2, 3, 28, 29, 30, 31)):
                pack_ref[pl.ds(base + place, 1), :] = rows_ref[kind, pl.ds(c, 1), :]
            for g in range(3):
                for h in range(2):
                    some = [
                        spread_row(rows_ref[kind, pl.ds(2 * (2 + 4 * g + j) + h, 1), :]) for j in range(4)
                    ]
                    pack_ref[pl.ds(base + 8 + 2 * g + h, 1), :] = gather_blocks(some)[:1]
        lane = iota(1)
        speeds = jnp.zeros((8, 128), f32)
        for k in range(4 * STEPS):
            speeds = jnp.where(lane == k, flow_ref[(k // 4 * L + level) * 4 + k % 4], speeds)
        pack_ref[pl.ds(3 * LINES, 1), :] = speeds[:1]
        pack_ref[pl.ds(3 * LINES + 1, EXTRA - 3 * LINES - 1), :] = jnp.zeros(
            (EXTRA - 3 * LINES - 1, 128), f32
        )
        for member in range(members):
            for k in range(EXTRA // 8):
                out_ref[member, pl.ds(FRAME + 8 * k, 8), :] = pack_ref[pl.ds(8 * k, 8), :]


def set_ghosts(ends, sides, first, last, seam_ref, side_ref):
    low = iota(1) < S
    for q in range(8):
        seam_ref[pl.ds(8 * q, 8), :] = jnp.where(low, ends[q], turn(last[q], S))
        seam_ref[pl.ds(S + 8 * q, 8), :] = jnp.where(low, turn(first[q], S), ends[q])
    for q in range(4):
        side_ref[pl.ds(8 * q, 8), :] = jnp.where(low, sides[q], turn(sides[q + 4], S))
        side_ref[pl.ds(ROWS + 8 * q, 8), :] = jnp.where(low, turn(sides[q], S), sides[q + 4])


def edge_rows(field_ref):
    first = [field_ref[0, pl.ds(8 * q, 8), :] for q in range(8)]
    last = [field_ref[ROWS - 1, pl.ds(8 * q, 8), :] for q in range(8)]
    return first, last


def sweep_rows(adjoint, field_ref, state_ref, rate_ref, seam_ref, side_ref):
    head, tail = iota(0) == 0, iota(0) == 7
    before = [seam_ref[pl.ds(8 * q, 8), :] for q in range(8)]
    here = [field_ref[0, pl.ds(8 * q, 8), :] for q in range(8)]
    for r in range(ROWS):
        if r < ROWS - 1:
            after = [field_ref[r + 1, pl.ds(8 * q, 8), :] for q in range(8)]
        else:
            after = [seam_ref[pl.ds(S + 8 * q, 8), :] for q in range(8)]
        outer = spread_row(side_ref[pl.ds(r, 1), :])
        down = [pltpu.roll(here[q], 1, 0) for q in range(8)]
        up = [pltpu.roll(here[q], 7, 0) for q in range(8)]
        closing = spread_row(side_ref[pl.ds(ROWS + r, 1), :])
        for q in range(8):
            cells = pl.ds(8 * q, 8)
            left = jnp.where(head, outer if q == 0 else down[q - 1], down[q])
            right = jnp.where(tail, closing if q == 7 else up[q + 1], up[q])
            change = (before[q] + after[q]) + (left + right) - 4.0 * here[q]
            if adjoint:
                state = state_ref[r, cells, :] + change
                state_ref[r, cells, :] = state
                field_ref[r, cells, :] = state * rate_ref[r, cells, :]
            else:
                field_ref[r, cells, :] = here[q] + rate_ref[r, cells, :] * change
        before, here = here, after


def scale_rows(field_ref, state_ref, rate_ref):
    def scale(r, carry):
        field_ref[r] = state_ref[r] * rate_ref[r]
        return carry

    lax.fori_loop(0, ROWS, scale, 0, unroll=4)


def pair_line(x_ref, i):
    lower = iota(0) < 4
    out = []
    for pair in range(PAIRS):
        a = x_ref[2 * pair, pl.ds(8 * (i // 2), 8), :]
        b = x_ref[2 * pair + 1, pl.ds(8 * (i // 2), 8), :]
        out.append(jnp.where(lower, a, swap(b)) if i % 2 == 0 else jnp.where(lower, swap(a), b))
    return out


def unpack_columns(line, put, get):
    low = iota(1) < S

    def turned(first, second):
        return jnp.transpose(jnp.concatenate(line(first) + line(second), axis=0))

    def part(block, start):
        start %= 128
        return block[start : start + 8]

    for c in range(4):
        block = turned(c, 4 + c)
        for parity in range(2):
            for q in range(8):
                put(2 * c + parity, q, part(block, S * parity + 8 * q))
                put(24 + 2 * c + parity, q, part(block, S * parity + 8 * q))
    starts = {(0, 0): 0, (1, 0): 64, (0, 7): 56, (1, 7): 120}
    for h in range(2):
        block = turned(8 + h, 12 + h)
        for j in range(4):
            for (parity, q), start in starts.items():
                put(8 + 4 * j + 2 * h + parity, q, part(block, start + 16 * j))
        block = turned(10 + h, 10 + h)
        for j in range(4):
            for (parity, q), start in starts.items():
                cells = part(block, start + 16 * j)
                if j < 2:
                    r = 24 + 4 * j + 2 * h + parity
                    put(r, q, jnp.where(low, cells, get(r, q)))
                else:
                    r = 4 * (j - 2) + 2 * h + parity
                    put(r, q, jnp.where(low, get(r, q), cells))


def frame_kernel(adjoint, table_ref, x_ref, *refs):
    if adjoint:
        rate_ref, out_ref, field_ref, seam_ref, side_ref, state_ref = refs
    else:
        out_ref, rate_ref, target_ref, speed_ref, field_ref, seam_ref, side_ref = refs
        state_ref = None
    lower = iota(0) < 4
    low = iota(1) < S
    zero = jnp.zeros((8, 128), f32)

    def access(ref):
        def put(r, q, value):
            ref[r, pl.ds(8 * q, 8), :] = value

        return put, lambda r, q: ref[r, pl.ds(8 * q, 8), :]

    def clear(ref):
        for r in range(8, 24):
            for q in range(1, 7):
                ref[r, pl.ds(8 * q, 8), :] = zero

    def field_line(i):
        return pair_line(x_ref, i)

    def rate_line(i):
        out = []
        for pair in range(PAIRS):
            a = x_ref[2 * pair, pl.ds(FRAME + i, 1), :]
            b = x_ref[2 * pair + 1, pl.ds(FRAME + i, 1), :]
            out.append(jnp.where(lower, spread_row(a), spread_row(b)))
        return out

    start_ref = state_ref if adjoint else field_ref
    clear(start_ref)
    unpack_columns(field_line, *access(start_ref))
    if adjoint:
        scale_rows(field_ref, state_ref, rate_ref)
    else:
        clear(rate_ref)
        unpack_columns(rate_line, *access(rate_ref))

    def place(repeat):
        first, last = edge_rows(field_ref)
        ends = [jnp.where(low, first[q], last[q]) for q in range(8)]
        left = [field_ref[pl.ds(8 * q, 8), 0, :] for q in range(4)]
        right = [field_ref[pl.ds(8 * q, 8), S - 1, :] for q in range(4)]
        sides = [jnp.where(low, left[q], turn(right[q], S)) for q in range(4)]
        sides += [jnp.where(low, turn(left[q], S), right[q]) for q in range(4)]
        mirror = 7 - iota(0)
        found = []
        for k in range(2):
            index, kind, flip = table_ref[k, 0], table_ref[k, 1], table_ref[k, 2]
            got = [jnp.where(kind != 0, pick(sides[q], index), pick(ends[q], index)) for q in range(8)]
            back = [
                jnp.take_along_axis(got[7 - q], mirror, axis=0, mode="promise_in_bounds")
                for q in range(8)
            ]
            found.append([jnp.where(flip != 0, back[q], got[q]) for q in range(8)])
        ends, sides = found
        set_ghosts(ends, sides, first, last, seam_ref, side_ref)
        block = jnp.transpose(jnp.concatenate(ends + sides, axis=0))
        line = pl.ds(pl.multiple_of(8 * repeat, 8), 8)
        for pair in range(PAIRS):
            a = block[8 * pair : 8 * pair + 8]
            b = block[S + 8 * pair : S + 8 * pair + 8]
            out_ref[2 * pair, line, :] = jnp.where(lower, a, swap(b))
            out_ref[2 * pair + 1, line, :] = jnp.where(lower, swap(a), b)

    def sweep(repeat, carry):
        place(repeat)
        sweep_rows(adjoint, field_ref, state_ref, rate_ref, seam_ref, side_ref)
        return carry

    lax.fori_loop(0, SWEEPS - 1, sweep, 0)
    place(SWEEPS - 1)

    if not adjoint:
        for group in range(2):
            tiles = pl.ds(8 * group, 8)
            for kind in range(2):
                start = FRAME + LINES + kind * LINES
                cells = split_halves(unpack([x_ref[tiles, start + i, :] for i in range(LINES)]))
                for r in range(ROWS):
                    target_ref[kind, group, r] = cells[r]
            speeds = x_ref[tiles, FRAME + 3 * LINES, :]
            for k in range(4 * STEPS):
                speed_ref[group, k] = jnp.broadcast_to(speeds[:, k : k + 1], (8, 128))


def load_columns(line, ref):
    for c in range(ROWS // 2):
        block = jnp.transpose(jnp.concatenate(line(c) + line(c + ROWS // 2), axis=0))
        for parity in range(2):
            ref[2 * c + parity] = block[S * parity : S * parity + S]


def rate_kernel(rows_ref, out_ref):
    load_columns(lambda c: [spread_row(rows_ref[0, pl.ds(c, 1), :])] * PAIRS, out_ref)


def tile_kernel(adjoint, x_ref, series_ref, rate_ref, *refs):
    if adjoint:
        added_ref, out_ref, field_ref, seam_ref, side_ref, state_ref = refs
    else:
        out_ref, field_ref, seam_ref, side_ref = refs
        state_ref = None
    lower = iota(0) < 4
    result_ref = state_ref if adjoint else field_ref
    load_columns(lambda c: pair_line(x_ref, c), result_ref)
    if adjoint:
        scale_rows(field_ref, state_ref, rate_ref)

    def sweep(repeat, carry):
        line = pl.ds(pl.multiple_of(8 * repeat, 8), 8)
        near, far = [], []
        for pair in range(PAIRS):
            one, other = pair_cells([series_ref[2 * pair, line, :]], [series_ref[2 * pair + 1, line, :]])
            near.append(one)
            far.append(other)
        block = jnp.transpose(jnp.concatenate(near + far, axis=0))
        ends = [block[8 * q : 8 * q + 8] for q in range(8)]
        sides = [block[S + 8 * q : S + 8 * q + 8] for q in range(8)]
        set_ghosts(ends, sides, *edge_rows(field_ref), seam_ref, side_ref)
        sweep_rows(adjoint, field_ref, state_ref, rate_ref, seam_ref, side_ref)
        return carry

    lax.fori_loop(0, SWEEPS, sweep, 0)

    for k in range(ROWS // 4):
        even, odd = [
            jnp.transpose(jnp.concatenate([result_ref[2 * c], result_ref[2 * c + 1]], axis=0))
            for c in (2 * k, 2 * k + 1)
        ]
        for half in range(2):
            line = pl.ds(8 * k + FIELD // 2 * half, 8)
            for pair in range(PAIRS):
                start = S * half + 8 * pair
                a, b = even[start : start + 8], odd[start : start + 8]
                a, b = jnp.where(lower, a, swap(b)), jnp.where(lower, swap(a), b)
                if adjoint:
                    a = a + added_ref[2 * pair, line, :]
                    b = b + added_ref[2 * pair + 1, line, :]
                out_ref[2 * pair, line, :] = a
                out_ref[2 * pair + 1, line, :] = b


VMEM = pl.BlockSpec(memory_space=pltpu.VMEM)
SMEM = pl.BlockSpec(memory_space=pltpu.SMEM)


def shape(*dims):
    return jax.ShapeDtypeStruct(dims, f32)


def pack_first(lines, own, flow, rate, weight, target):
    return pl.pallas_call(
        pack_kernel,
        out_shape=(shape(lines.shape[0], FRAME + EXTRA, 128), shape(3, ROWS, 128)),
        in_specs=[VMEM, SMEM, SMEM, VMEM, VMEM, VMEM],
        out_specs=(VMEM, VMEM),
        scratch_shapes=[pltpu.VMEM((EXTRA, 128), f32)],
        name="pack_first",
    )(lines, own, flow, rate, weight, target)


def pack(lines):
    return pl.pallas_call(
        pack_kernel,
        out_shape=shape(lines.shape[0], FRAME, 128),
        in_specs=[VMEM],
        out_specs=VMEM,
        name="pack",
    )(lines)


FIELDS = pltpu.VMEM((ROWS, S, 128), f32)
FRAME_SCRATCH = [FIELDS, pltpu.VMEM((2 * S, 128), f32), pltpu.VMEM((2 * ROWS, 128), f32)]


def frame_forward(table, received):
    return pl.pallas_call(
        functools.partial(frame_kernel, False),
        out_shape=(
            shape(TILES, SERIES, 128),
            shape(ROWS, S, 128),
            shape(2, 2, ROWS, 8, 128),
            shape(2, 4 * STEPS, 8, 128),
        ),
        in_specs=[VMEM, VMEM],
        out_specs=(VMEM, VMEM, VMEM, VMEM),
        scratch_shapes=FRAME_SCRATCH,
        name="frame_forward",
    )(table, received)


def frame_adjoint(table, received, rate):
    return pl.pallas_call(
        functools.partial(frame_kernel, True),
        out_shape=shape(TILES, SERIES, 128),
        in_specs=[VMEM, VMEM, VMEM],
        out_specs=VMEM,
        scratch_shapes=FRAME_SCRATCH + [FIELDS],
        name="frame_adjoint",
    )(table, received, rate)


def spread_rate(rows):
    return pl.pallas_call(
        rate_kernel,
        out_shape=shape(ROWS, S, 128),
        in_specs=[VMEM],
        out_specs=VMEM,
        cost_estimate=pl.CostEstimate(flops=2_000_000, bytes_accessed=1_100_000, transcendentals=0),
        name="spread_rate",
    )(rows)


def tile_smooth(adjoint, lines, series, rate, *added):
    return pl.pallas_call(
        functools.partial(tile_kernel, adjoint),
        out_shape=shape(lines.shape[0], FIELD, 128),
        in_specs=[VMEM] * (3 + len(added)),
        out_specs=VMEM,
        scratch_shapes=FRAME_SCRATCH + [FIELDS] * adjoint,
        name="tile_adjoint" if adjoint else "tile_forward",
    )(lines, series, rate, *added)


def transport_kernel(
    src_ref,
    own_ref,
    flip_ref,
    x_ref,
    target_ref,
    speed_ref,
    rows_ref,
    out_ref,
    field_ref,
    strip_ref,
    ghost_ref,
    plain_ref,
    mine_ref,
):
    low = iota(1) < S
    column = iota(1) % S
    mask = edge_mask()

    def save_strips(group, strips):
        for edge in range(4):
            strip_ref[pl.ds(edge * TILES + 8 * group, 8), :] = strips[edge]

    def fetch():
        for tile in range(TILES):
            for d in range(4):
                ghost_ref[pl.ds(d * TILES + tile, 1), :] = strip_ref[pl.ds(src_ref[4 * tile + d], 1), :]

    def step(section, adjoint):
        for group in range(2):
            values = [field_ref[group, r] for r in range(ROWS)]
            strips = strips_of(values[0], values[-1], column_sum(values))
            if adjoint:
                strips = [strips[d] * speed_ref[group, 4 * section + d] for d in range(4)]
            save_strips(group, strips)
        fetch()
        for group in range(2):
            c = [speed_ref[group, 4 * section + d] for d in range(4)]
            keep = 1.0 - ((c[0] + c[1]) + (c[2] + c[3]))
            tiles = [pl.ds(d * TILES + 8 * group, 8) for d in range(4)]
            ghosts = [ghost_ref[tiles[d], :] for d in range(4)]
            if not adjoint:
                ghosts = [ghosts[d] * c[d] for d in range(4)]
            else:
                c = [c[1], c[0], c[3], c[2]]
            flips = [flip_ref[tiles[d], :] for d in range(4)]
            top, bottom, sides = placed_ghosts(ghosts, flips)
            first = field_ref[group, 0]
            last = field_ref[group, ROWS - 1]
            owned = iota(0) + 8 * group == own_ref[0]
            previous = None
            here = first
            for r in range(ROWS):
                after = field_ref[group, r + 1] if r < ROWS - 1 else None
                side = turn(sides, -2 * r)
                left = jnp.where(column == 0, side, c[2] * turn(here, 1))
                right = jnp.where(column == S - 1, side, c[3] * turn(here, -1))
                if r == 0:
                    up = jnp.where(low, top, c[0] * turn(last, S))
                else:
                    up = c[0] * previous
                if r == ROWS - 1:
                    down = jnp.where(low, c[1] * turn(first, S), bottom)
                else:
                    down = c[1] * after
                new = keep * here + (up + down) + (left + right)
                if section == STEPS - 1 and not adjoint:
                    weight = jnp.where(owned, mine_ref[0, r], target_ref[0, group, r])
                    goal = jnp.where(owned, mine_ref[1, r], target_ref[1, group, r])
                    new = weight * (new - goal)
                field_ref[group, r] = new
                previous, here = here, after

    for kind in range(2):
        rows = split_halves([spread_row(rows_ref[kind + 1, pl.ds(c, 1), :]) for c in range(ROWS)])
        for r in range(ROWS):
            mine_ref[kind, r] = rows[r]
    for group in range(2):
        rows = split_halves([x_ref[pl.ds(8 * group, 8), c, :] for c in range(ROWS)])
        for r in range(ROWS):
            field_ref[group, r] = rows[r]
    for section in range(STEPS):
        step(section, False)
    for section in reversed(range(STEPS)):
        step(section, True)
    for group in range(2):
        cells = join_halves([field_ref[group, r] for r in range(ROWS)])
        for c in range(ROWS):
            plain_ref[pl.ds(8 * group, 8), c, :] = cells[c]
    mine = plain_ref[own_ref[0]]
    for other in range(out_ref.shape[0]):
        out_ref[other] = mine


def transport(src, own, flip, gathered, target, speed, rows, copies):
    return pl.pallas_call(
        transport_kernel,
        out_shape=shape(copies, ROWS, 128),
        in_specs=[SMEM, SMEM] + [VMEM] * 5,
        out_specs=VMEM,
        scratch_shapes=[
            pltpu.VMEM((2, ROWS, 8, 128), f32),
            pltpu.VMEM((4 * TILES, 128), f32),
            pltpu.VMEM((4 * TILES, 128), f32),
            pltpu.VMEM((TILES, ROWS, 128), f32),
            pltpu.VMEM((2, ROWS, 8, 128), f32),
        ],
        name="transport",
    )(src, own, flip, gathered, target, speed, rows)


def exchange(values, axis):
    return lax.all_to_all(values, axis, split_axis=0, concat_axis=0, tiled=True)


def to_lines(fields):
    lead = fields.shape[:-2]
    fields = fields.reshape(*lead, L, ROWS, 128)
    return jnp.swapaxes(fields, -3, -2).reshape(*lead, FIELD, 128)


def from_lines(lines):
    lead = lines.shape[:-2]
    lines = lines.reshape(*lead, ROWS, L, 128)
    return jnp.swapaxes(lines, -3, -2).reshape(*lead, L, ROWS * 128)


def body(
    control,
    perturbations,
    diffusivity,
    flow,
    observed,
    obs_weight,
    neighbour_tile,
    neighbour_edge,
    departure,
):
    source = (neighbour_edge * TILES + neighbour_tile).reshape(-1)
    flips = (departure[:, :, 0] != 0).astype(jnp.int32) * S

    def by_lane(values):
        return jnp.repeat(values.T.reshape(2, 2 * TILES), L, axis=1)

    place = (neighbour_edge % 2) * S + neighbour_tile * L
    index = by_lane(place) + jnp.arange(128, dtype=jnp.int32) % L
    table = jnp.stack([index, by_lane(neighbour_edge // 2), by_lane(flips)], axis=1)
    table = jnp.broadcast_to(table[:, :, None], (2, 3, 8, 128))
    flip = jnp.broadcast_to(flips.T.reshape(4 * TILES, 1), (4 * TILES, 128))
    own = lax.axis_index("tile").reshape(1)
    row = lax.axis_index("member")
    control_lines = to_lines(control[:, 0])

    packed, rows = pack_first(
        control_lines,
        jnp.stack([row // L, row % L]),
        flow.reshape(-1),
        diffusivity.reshape(ROWS, 128),
        to_lines(obs_weight[0]),
        to_lines(observed[0]),
    )
    own_rate = spread_rate(rows)
    received = exchange(packed, "tile")
    series, rate, goal, speed = frame_forward(table, received)
    smoothed = tile_smooth(False, control_lines, exchange(series, "tile"), own_rate)

    spread = to_lines(perturbations[:, 0])
    partial = jnp.sum(spread * smoothed[:, None], axis=0)
    partial = jnp.swapaxes(partial.reshape(V, ROWS, L, 128), 1, 2).reshape(V * L, ROWS, 128)
    increment = jnp.sum(exchange(partial, "member"), axis=0)
    gathered = exchange(jnp.broadcast_to(increment[None], (TILES, ROWS, 128)), "tile")
    sensitivity = transport(source, own, flip, gathered, goal, speed, rows, V * L)
    sensitivity = exchange(sensitivity, "member")
    sensitivity = jnp.swapaxes(sensitivity.reshape(V, L, ROWS, 128), 1, 2).reshape(V, FIELD, 128)

    projected = jnp.sum(spread * sensitivity[None], axis=1)
    series = frame_adjoint(table, exchange(pack(projected), "tile"), rate)
    mixed = tile_smooth(True, projected, exchange(series, "tile"), own_rate, control_lines)
    return from_lines(mixed)[:, None]


def solution(mesh):
    in_specs = (
        P("member", "tile", None, None),
        P("member", "tile", None, None, None),
        P("tile", None),
        P(None, "tile", None, None),
        P("tile", None, None, None),
        P("tile", None, None, None),
        P(),
        P(),
        P(),
    )
    out_specs = P("member", "tile", None, None)
    return jax.shard_map(body, mesh=mesh, in_specs=in_specs, out_specs=out_specs, check_vma=False)
```

```python
import functools

import jax
import jax.numpy as jnp
from jax import lax
from jax.experimental import pallas as pl
from jax.experimental.pallas import tpu as pltpu
from jax.sharding import PartitionSpec as P

S = 64
V = 4
L = 4
SWEEPS = 8
STEPS = 2
TILES = 16
PAIRS = TILES // 2
ROWS = 32
GROUP = 4
FIELD = L * ROWS
LINES = 14
FRAME = L * LINES
SERIES = 8 * SWEEPS
SHALLOW = 4
EXTRA = 24
f32 = jnp.float32


def iota(axis):
    return lax.broadcasted_iota(jnp.int32, (8, 128), axis)


def turn(x, shift):
    shift %= 128
    return pltpu.roll(x, shift, 1) if shift else x


def swap(x):
    return pltpu.roll(x, 4, 0)


def pick(x, index):
    return jnp.take_along_axis(x, index, axis=1, mode="promise_in_bounds")


def split_halves(cells):
    low = iota(1) < S
    out = []
    for c in range(ROWS // 2):
        first, second = cells[c], cells[c + ROWS // 2]
        out.append(jnp.where(low, first, turn(second, S)))
        out.append(jnp.where(low, turn(first, S), second))
    return out


def join_halves(rows):
    low = iota(1) < S
    out = [None] * ROWS
    for c in range(ROWS // 2):
        even, odd = rows[2 * c], rows[2 * c + 1]
        out[c] = jnp.where(low, even, turn(odd, S))
        out[c + ROWS // 2] = jnp.where(low, turn(even, S), odd)
    return out


def edge_mask():
    column = iota(1) % S
    return (column == 0) | (column == S - 1)


def column_sum(values):
    mask = edge_mask()
    parts = [turn(jnp.where(mask, values[r], 0.0), 2 * r) for r in range(ROWS)]
    while len(parts) > 1:
        parts = [a + b for a, b in zip(parts[0::2], parts[1::2])]
    return parts[0]


def strips_of(top, bottom, columns):
    lane = iota(1)
    place = jnp.where(lane < S, lane, 127 - lane)
    return (
        pick(top, place),
        pick(bottom, place + S),
        pick(columns, 2 * place),
        pick(columns, (2 * place + 63) % 128),
    )


def placed_ghosts(ghosts, flips):
    lane = iota(1)
    even = lane % 2 == 0
    along = lane % S
    top = pick(ghosts[0], along + flips[0])
    bottom = pick(ghosts[1], along + flips[1])
    left = pick(ghosts[2], lane // 2 + flips[2])
    right = pick(ghosts[3], ((lane + 65) % 128) // 2 + flips[3])
    return top, bottom, jnp.where(even, left, right)


def gather_blocks(cells):
    lane = iota(1)
    packed = cells[0]
    for j in range(1, 4):
        packed = jnp.where((lane + 8 - 16 * j) % S < 16, turn(cells[j], 16 * j), packed)
    return packed


def gather_corners(cells):
    lane = iota(1)
    packed = cells[0]
    for j in range(1, 16):
        packed = jnp.where((lane + 2 - 4 * j) % S < 4, turn(cells[j], 4 * j), packed)
    return packed


def unpack_shallow(lines):
    out = [turn(lines[2 + c // 16], -4 * (c % 16)) for c in range(ROWS)]
    out[0], out[-1] = lines[0], lines[1]
    return out


def pair_cells(a, b):
    lower = iota(0) < 4
    cells = []
    for x, y in zip(a, b):
        cells.append(jnp.where(lower, x, swap(y)))
        cells.append(jnp.where(lower, swap(x), y))
    return cells


def spread_row(row):
    return jnp.broadcast_to(row, (8, 128))


def pack_frame(cells, out_ref, member):
    for place, k in enumerate((0, 1, 14, 15)):
        out_ref[member, pl.ds(8 * place, 8), :] = cells[k]
    for g in range(3):
        out_ref[member, pl.ds(32 + 8 * g, 8), :] = gather_blocks(cells[2 + 4 * g : 6 + 4 * g])


def pack_kernel(x_ref, flow_ref, rate_ref, weight_ref, target_ref, out_ref, rows_ref, pack_ref):
    members = x_ref.shape[0]

    def one(member, carry):
        cells = [x_ref[member, pl.ds(8 * k, 8), :] for k in range(ROWS // 2)]
        pack_frame(cells, out_ref, member)
        return carry

    lax.fori_loop(0, members, one, 0, unroll=8)
    row = lax.axis_index("member")
    variable, level = row // L, row % L
    for c in range(ROWS):
        line = pl.ds(L * c + level, 1)
        rows_ref[0, pl.ds(c, 1), :] = rate_ref[pl.ds(c, 1), :]
        rows_ref[1, pl.ds(c, 1), :] = weight_ref[variable, line, :]
        rows_ref[2, pl.ds(c, 1), :] = target_ref[variable, line, :]

    def spread(kind, c):
        return spread_row(rows_ref[kind, pl.ds(c, 1), :])

    for place, c in enumerate((0, 1, 2, 3, 28, 29, 30, 31)):
        pack_ref[pl.ds(place, 1), :] = rows_ref[0, pl.ds(c, 1), :]
    for g in range(3):
        for h in range(2):
            some = [spread(0, 2 * (2 + 4 * g + j) + h) for j in range(4)]
            pack_ref[pl.ds(8 + 2 * g + h, 1), :] = gather_blocks(some)[:1]
    for kind in range(1, 3):
        base = LINES + (kind - 1) * SHALLOW
        pack_ref[pl.ds(base, 1), :] = rows_ref[kind, pl.ds(0, 1), :]
        pack_ref[pl.ds(base + 1, 1), :] = rows_ref[kind, pl.ds(ROWS - 1, 1), :]
        for half in range(2):
            some = [spread(kind, 16 * half + j) for j in range(16)]
            pack_ref[pl.ds(base + 2 + half, 1), :] = gather_corners(some)[:1]
    lane = iota(1)
    speeds = jnp.zeros((8, 128), f32)
    for k in range(4 * STEPS):
        speeds = jnp.where(lane == k, flow_ref[k // 4, level, k % 4], speeds)
    base = LINES + 2 * SHALLOW
    pack_ref[pl.ds(base, 1), :] = speeds[:1]
    pack_ref[pl.ds(base + 1, EXTRA - base - 1), :] = jnp.zeros((EXTRA - base - 1, 128), f32)
    for member in range(members):
        for k in range(EXTRA // 8):
            out_ref[member, pl.ds(FRAME + 8 * k, 8), :] = pack_ref[pl.ds(8 * k, 8), :]


def increment_kernel(spread_ref, smoothed_ref, out_ref, total_ref):
    step = pl.program_id(0)

    @pl.when(step == 0)
    def _():
        total_ref[...] = jnp.zeros(total_ref.shape, f32)

    for k in range(FIELD // 8):
        line = pl.ds(8 * k, 8)
        fields = [smoothed_ref[m, line, :] for m in range(GROUP)]
        for v in range(V):
            terms = [spread_ref[m, v, line, :] * fields[m] for m in range(GROUP)]
            while len(terms) > 1:
                terms = [a + b for a, b in zip(terms[0::2], terms[1::2])]
            total_ref[v, line, :] = total_ref[v, line, :] + terms[0]

    @pl.when(step == pl.num_programs(0) - 1)
    def _():
        for v in range(V):
            for c in range(ROWS):
                out_ref[pl.ds(L * v, L), c, :] = total_ref[v, pl.ds(L * c, L), :]


def project_kernel(spread_ref, rows_ref, out_ref, frame_ref, lines_ref):
    @pl.when(pl.program_id(0) == 0)
    def _():
        for v in range(V):
            for c in range(ROWS):
                lines_ref[v, pl.ds(L * c, L), :] = rows_ref[pl.ds(L * v, L), c, :]

    for k in range(FIELD // 8):
        line = pl.ds(8 * k, 8)
        fields = [lines_ref[v, line, :] for v in range(V)]
        for m in range(GROUP):
            terms = [spread_ref[m, v, line, :] * fields[v] for v in range(V)]
            value = (terms[0] + terms[1]) + (terms[2] + terms[3])
            out_ref[m, line, :] = value
    for m in range(GROUP):
        pack_frame([out_ref[m, pl.ds(8 * k, 8), :] for k in range(FIELD // 8)], frame_ref, m)


def set_ghosts(ends, sides, first, last, seam_ref, side_ref):
    low = iota(1) < S
    for q in range(8):
        seam_ref[pl.ds(8 * q, 8), :] = jnp.where(low, ends[q], turn(last[q], S))
        seam_ref[pl.ds(S + 8 * q, 8), :] = jnp.where(low, turn(first[q], S), ends[q])
    for q in range(4):
        side_ref[pl.ds(8 * q, 8), :] = jnp.where(low, sides[q], turn(sides[q + 4], S))
        side_ref[pl.ds(ROWS + 8 * q, 8), :] = jnp.where(low, turn(sides[q], S), sides[q + 4])


def edge_rows(field_ref):
    first = [field_ref[0, pl.ds(8 * q, 8), :] for q in range(8)]
    last = [field_ref[ROWS - 1, pl.ds(8 * q, 8), :] for q in range(8)]
    return first, last


def sweep_rows(adjoint, field_ref, state_ref, rate_ref, seam_ref, side_ref):
    head, tail = iota(0) == 0, iota(0) == 7
    before = [seam_ref[pl.ds(8 * q, 8), :] for q in range(8)]
    here = [field_ref[0, pl.ds(8 * q, 8), :] for q in range(8)]
    for r in range(ROWS):
        if r < ROWS - 1:
            after = [field_ref[r + 1, pl.ds(8 * q, 8), :] for q in range(8)]
        else:
            after = [seam_ref[pl.ds(S + 8 * q, 8), :] for q in range(8)]
        outer = spread_row(side_ref[pl.ds(r, 1), :])
        down = [pltpu.roll(here[q], 1, 0) for q in range(8)]
        up = [pltpu.roll(here[q], 7, 0) for q in range(8)]
        closing = spread_row(side_ref[pl.ds(ROWS + r, 1), :])
        for q in range(8):
            cells = pl.ds(8 * q, 8)
            left = jnp.where(head, outer if q == 0 else down[q - 1], down[q])
            right = jnp.where(tail, closing if q == 7 else up[q + 1], up[q])
            change = (before[q] + after[q]) + (left + right) - 4.0 * here[q]
            if adjoint:
                state = state_ref[r, cells, :] + change
                state_ref[r, cells, :] = state
                field_ref[r, cells, :] = state * rate_ref[r, cells, :]
            else:
                field_ref[r, cells, :] = here[q] + rate_ref[r, cells, :] * change
        before, here = here, after


def scale_rows(field_ref, state_ref, rate_ref):
    def scale(r, carry):
        field_ref[r] = state_ref[r] * rate_ref[r]
        return carry

    lax.fori_loop(0, ROWS, scale, 0, unroll=4)


def pair_line(x_ref, i):
    lower = iota(0) < 4
    out = []
    for pair in range(PAIRS):
        a = x_ref[2 * pair, pl.ds(8 * (i // 2), 8), :]
        b = x_ref[2 * pair + 1, pl.ds(8 * (i // 2), 8), :]
        out.append(jnp.where(lower, a, swap(b)) if i % 2 == 0 else jnp.where(lower, swap(a), b))
    return out


def unpack_columns(line, put, get):
    low = iota(1) < S

    def turned(first, second):
        return jnp.transpose(jnp.concatenate(line(first) + line(second), axis=0))

    def part(block, start):
        start %= 128
        return block[start : start + 8]

    for c in range(4):
        block = turned(c, 4 + c)
        for parity in range(2):
            for q in range(8):
                put(2 * c + parity, q, part(block, S * parity + 8 * q))
                put(24 + 2 * c + parity, q, part(block, S * parity + 8 * q))
    starts = {(0, 0): 0, (1, 0): 64, (0, 7): 56, (1, 7): 120}
    for h in range(2):
        block = turned(8 + h, 12 + h)
        for j in range(4):
            for (parity, q), start in starts.items():
                put(8 + 4 * j + 2 * h + parity, q, part(block, start + 16 * j))
        block = turned(10 + h, 10 + h)
        for j in range(4):
            for (parity, q), start in starts.items():
                cells = part(block, start + 16 * j)
                if j < 2:
                    r = 24 + 4 * j + 2 * h + parity
                    put(r, q, jnp.where(low, cells, get(r, q)))
                else:
                    r = 4 * (j - 2) + 2 * h + parity
                    put(r, q, jnp.where(low, get(r, q), cells))


def frame_kernel(adjoint, table_ref, x_ref, *refs):
    if adjoint:
        rate_ref, out_ref, field_ref, seam_ref, side_ref, state_ref = refs
    else:
        out_ref, rate_ref, target_ref, speed_ref, field_ref, seam_ref, side_ref = refs
        state_ref = None
    lower = iota(0) < 4
    low = iota(1) < S
    zero = jnp.zeros((8, 128), f32)

    def access(ref):
        def put(r, q, value):
            ref[r, pl.ds(8 * q, 8), :] = value

        return put, lambda r, q: ref[r, pl.ds(8 * q, 8), :]

    def clear(ref):
        for r in range(8, 24):
            for q in range(1, 7):
                ref[r, pl.ds(8 * q, 8), :] = zero

    def field_line(i):
        return pair_line(x_ref, i)

    def rate_line(i):
        out = []
        for pair in range(PAIRS):
            a = x_ref[2 * pair, pl.ds(FRAME + i, 1), :]
            b = x_ref[2 * pair + 1, pl.ds(FRAME + i, 1), :]
            out.append(jnp.where(lower, spread_row(a), spread_row(b)))
        return out

    start_ref = state_ref if adjoint else field_ref
    clear(start_ref)
    unpack_columns(field_line, *access(start_ref))
    if adjoint:
        scale_rows(field_ref, state_ref, rate_ref)
    else:
        clear(rate_ref)
        unpack_columns(rate_line, *access(rate_ref))

    def place(repeat):
        first, last = edge_rows(field_ref)
        ends = [jnp.where(low, first[q], last[q]) for q in range(8)]
        left = [field_ref[pl.ds(8 * q, 8), 0, :] for q in range(4)]
        right = [field_ref[pl.ds(8 * q, 8), S - 1, :] for q in range(4)]
        sides = [jnp.where(low, left[q], turn(right[q], S)) for q in range(4)]
        sides += [jnp.where(low, turn(left[q], S), right[q]) for q in range(4)]
        mirror = 7 - iota(0)
        found = []
        for k in range(2):
            index, kind, flip = [spread_row(table_ref[pl.ds(3 * k + i, 1), :]) for i in range(3)]
            got = [jnp.where(kind != 0, pick(sides[q], index), pick(ends[q], index)) for q in range(8)]
            back = [
                jnp.take_along_axis(got[7 - q], mirror, axis=0, mode="promise_in_bounds")
                for q in range(8)
            ]
            found.append([jnp.where(flip != 0, back[q], got[q]) for q in range(8)])
        ends, sides = found
        set_ghosts(ends, sides, first, last, seam_ref, side_ref)
        block = jnp.transpose(jnp.concatenate(ends + sides, axis=0))
        line = pl.ds(pl.multiple_of(8 * repeat, 8), 8)
        for pair in range(PAIRS):
            a = block[8 * pair : 8 * pair + 8]
            b = block[S + 8 * pair : S + 8 * pair + 8]
            out_ref[2 * pair, line, :] = jnp.where(lower, a, swap(b))
            out_ref[2 * pair + 1, line, :] = jnp.where(lower, swap(a), b)

    def sweep(repeat, carry):
        place(repeat)
        sweep_rows(adjoint, field_ref, state_ref, rate_ref, seam_ref, side_ref)
        return carry

    lax.fori_loop(0, SWEEPS - 1, sweep, 0)
    place(SWEEPS - 1)

    if not adjoint:
        for group in range(2):
            tiles = pl.ds(8 * group, 8)
            for kind in range(2):
                start = FRAME + LINES + kind * SHALLOW
                lines = [x_ref[tiles, start + i, :] for i in range(SHALLOW)]
                cells = split_halves(unpack_shallow(lines))
                for r in range(ROWS):
                    target_ref[kind, group, r] = cells[r]
            speeds = x_ref[tiles, FRAME + LINES + 2 * SHALLOW, :]
            for k in range(4 * STEPS):
                speed_ref[group, k] = jnp.broadcast_to(speeds[:, k : k + 1], (8, 128))


def load_columns(line, ref):
    for c in range(ROWS // 2):
        block = jnp.transpose(jnp.concatenate(line(c) + line(c + ROWS // 2), axis=0))
        for parity in range(2):
            ref[2 * c + parity] = block[S * parity : S * parity + S]


def rate_kernel(rows_ref, out_ref):
    load_columns(lambda c: [spread_row(rows_ref[0, pl.ds(c, 1), :])] * PAIRS, out_ref)


def tile_kernel(adjoint, x_ref, series_ref, rate_ref, *refs):
    if adjoint:
        added_ref, out_ref, field_ref, seam_ref, side_ref, state_ref = refs
    else:
        out_ref, field_ref, seam_ref, side_ref = refs
        state_ref = None
    lower = iota(0) < 4
    result_ref = state_ref if adjoint else field_ref
    load_columns(lambda c: pair_line(x_ref, c), result_ref)
    if adjoint:
        scale_rows(field_ref, state_ref, rate_ref)

    def sweep(repeat, carry):
        line = pl.ds(pl.multiple_of(8 * repeat, 8), 8)
        near, far = [], []
        for pair in range(PAIRS):
            one, other = pair_cells([series_ref[2 * pair, line, :]], [series_ref[2 * pair + 1, line, :]])
            near.append(one)
            far.append(other)
        block = jnp.transpose(jnp.concatenate(near + far, axis=0))
        ends = [block[8 * q : 8 * q + 8] for q in range(8)]
        sides = [block[S + 8 * q : S + 8 * q + 8] for q in range(8)]
        set_ghosts(ends, sides, *edge_rows(field_ref), seam_ref, side_ref)
        sweep_rows(adjoint, field_ref, state_ref, rate_ref, seam_ref, side_ref)
        return carry

    lax.fori_loop(0, SWEEPS, sweep, 0)

    for k in range(ROWS // 4):
        even, odd = [
            jnp.transpose(jnp.concatenate([result_ref[2 * c], result_ref[2 * c + 1]], axis=0))
            for c in (2 * k, 2 * k + 1)
        ]
        for half in range(2):
            line = pl.ds(8 * k + FIELD // 2 * half, 8)
            for pair in range(PAIRS):
                start = S * half + 8 * pair
                a, b = even[start : start + 8], odd[start : start + 8]
                a, b = jnp.where(lower, a, swap(b)), jnp.where(lower, swap(a), b)
                if adjoint:
                    a = a + added_ref[2 * pair, line, :]
                    b = b + added_ref[2 * pair + 1, line, :]
                out_ref[2 * pair, line, :] = a
                out_ref[2 * pair + 1, line, :] = b


GRANT = pltpu.CompilerParams(vmem_limit_bytes=16 * 1024 * 1024)
VMEM = pl.BlockSpec(memory_space=pltpu.VMEM)
SMEM = pl.BlockSpec(memory_space=pltpu.SMEM)


def shape(*dims):
    return jax.ShapeDtypeStruct(dims, f32)


def pack_first(lines, flow, rate, weight, target):
    return pl.pallas_call(
        pack_kernel,
        out_shape=(shape(lines.shape[0], FRAME + EXTRA, 128), shape(3, ROWS, 128)),
        in_specs=[VMEM, SMEM, VMEM, VMEM, VMEM],
        out_specs=(VMEM, VMEM),
        scratch_shapes=[pltpu.VMEM((EXTRA, 128), f32)],
        name="pack_first",
    )(lines, flow, rate, weight, target)


def members_block(*dims):
    return pl.BlockSpec((GROUP, *dims), lambda i: (i,) + (0,) * len(dims))


def whole_block(*dims):
    return pl.BlockSpec(dims, lambda i: (0,) * len(dims))


def increments(spread, smoothed):
    return pl.pallas_call(
        increment_kernel,
        grid=(spread.shape[0] // GROUP,),
        out_shape=shape(V * L, ROWS, 128),
        in_specs=[members_block(V, FIELD, 128), members_block(FIELD, 128)],
        out_specs=whole_block(V * L, ROWS, 128),
        scratch_shapes=[pltpu.VMEM((V, FIELD, 128), f32)],
        compiler_params=GRANT,
        name="increments",
    )(spread, smoothed)


def project(spread, rows):
    members = spread.shape[0]
    return pl.pallas_call(
        project_kernel,
        grid=(members // GROUP,),
        out_shape=(shape(members, FIELD, 128), shape(members, FRAME, 128)),
        in_specs=[members_block(V, FIELD, 128), whole_block(V * L, ROWS, 128)],
        out_specs=(members_block(FIELD, 128), members_block(FRAME, 128)),
        scratch_shapes=[pltpu.VMEM((V, FIELD, 128), f32)],
        compiler_params=GRANT,
        name="project",
    )(spread, rows)


FIELDS = pltpu.VMEM((ROWS, S, 128), f32)
FRAME_SCRATCH = [FIELDS, pltpu.VMEM((2 * S, 128), f32), pltpu.VMEM((2 * ROWS, 128), f32)]


def frame_forward(table, received):
    return pl.pallas_call(
        functools.partial(frame_kernel, False),
        out_shape=(
            shape(TILES, SERIES, 128),
            shape(ROWS, S, 128),
            shape(2, 2, ROWS, 8, 128),
            shape(2, 4 * STEPS, 8, 128),
        ),
        in_specs=[VMEM, VMEM],
        out_specs=(VMEM, VMEM, VMEM, VMEM),
        scratch_shapes=FRAME_SCRATCH,
        compiler_params=GRANT,
        name="frame_forward",
    )(table, received)


def frame_adjoint(table, received, rate):
    return pl.pallas_call(
        functools.partial(frame_kernel, True),
        out_shape=shape(TILES, SERIES, 128),
        in_specs=[VMEM, VMEM, VMEM],
        out_specs=VMEM,
        scratch_shapes=FRAME_SCRATCH + [FIELDS],
        compiler_params=GRANT,
        name="frame_adjoint",
    )(table, received, rate)


def spread_rate(rows):
    return pl.pallas_call(
        rate_kernel,
        out_shape=shape(ROWS, S, 128),
        in_specs=[VMEM],
        out_specs=VMEM,
        cost_estimate=pl.CostEstimate(flops=2_000_000, bytes_accessed=1_100_000, transcendentals=0),
        compiler_params=GRANT,
        name="spread_rate",
    )(rows)


def tile_smooth(adjoint, lines, series, rate, *added):
    return pl.pallas_call(
        functools.partial(tile_kernel, adjoint),
        out_shape=shape(lines.shape[0], FIELD, 128),
        in_specs=[VMEM] * (3 + len(added)),
        out_specs=VMEM,
        scratch_shapes=FRAME_SCRATCH + [FIELDS] * adjoint,
        compiler_params=GRANT,
        name="tile_adjoint" if adjoint else "tile_forward",
    )(lines, series, rate, *added)


def transport_kernel(
    src_ref,
    flip_ref,
    x_ref,
    target_ref,
    speed_ref,
    rows_ref,
    out_ref,
    field_ref,
    strip_ref,
    ghost_ref,
    plain_ref,
    mine_ref,
):
    low = iota(1) < S
    column = iota(1) % S
    mask = edge_mask()

    def save_strips(group, strips):
        for edge in range(4):
            strip_ref[pl.ds(edge * TILES + 8 * group, 8), :] = strips[edge]

    def fetch():
        for tile in range(TILES):
            for d in range(4):
                ghost_ref[pl.ds(d * TILES + tile, 1), :] = strip_ref[pl.ds(src_ref[4 * tile + d], 1), :]

    def step(section, adjoint):
        for group in range(2):
            values = [field_ref[group, r] for r in range(ROWS)]
            strips = strips_of(values[0], values[-1], column_sum(values))
            if adjoint:
                strips = [strips[d] * speed_ref[group, 4 * section + d] for d in range(4)]
            save_strips(group, strips)
        fetch()
        for group in range(2):
            c = [speed_ref[group, 4 * section + d] for d in range(4)]
            keep = 1.0 - ((c[0] + c[1]) + (c[2] + c[3]))
            tiles = [pl.ds(d * TILES + 8 * group, 8) for d in range(4)]
            ghosts = [ghost_ref[tiles[d], :] for d in range(4)]
            if not adjoint:
                ghosts = [ghosts[d] * c[d] for d in range(4)]
            else:
                c = [c[1], c[0], c[3], c[2]]
            flips = [jnp.broadcast_to(flip_ref[tiles[d], :], (8, 128)) for d in range(4)]
            top, bottom, sides = placed_ghosts(ghosts, flips)
            first = field_ref[group, 0]
            last = field_ref[group, ROWS - 1]
            owned = iota(0) + 8 * group == lax.axis_index("tile")
            previous = None
            here = first
            for r in range(ROWS):
                after = field_ref[group, r + 1] if r < ROWS - 1 else None
                side = turn(sides, -2 * r)
                left = jnp.where(column == 0, side, c[2] * turn(here, 1))
                right = jnp.where(column == S - 1, side, c[3] * turn(here, -1))
                if r == 0:
                    up = jnp.where(low, top, c[0] * turn(last, S))
                else:
                    up = c[0] * previous
                if r == ROWS - 1:
                    down = jnp.where(low, c[1] * turn(first, S), bottom)
                else:
                    down = c[1] * after
                new = keep * here + (up + down) + (left + right)
                if section == STEPS - 1 and not adjoint:
                    weight = jnp.where(owned, mine_ref[0, r], target_ref[0, group, r])
                    goal = jnp.where(owned, mine_ref[1, r], target_ref[1, group, r])
                    new = weight * (new - goal)
                field_ref[group, r] = new
                previous, here = here, after

    for kind in range(2):
        rows = split_halves([spread_row(rows_ref[kind + 1, pl.ds(c, 1), :]) for c in range(ROWS)])
        for r in range(ROWS):
            mine_ref[kind, r] = rows[r]
    for group in range(2):
        rows = split_halves([x_ref[pl.ds(8 * group, 8), c, :] for c in range(ROWS)])
        for r in range(ROWS):
            field_ref[group, r] = rows[r]
    for section in range(STEPS):
        step(section, False)
    for section in reversed(range(STEPS)):
        step(section, True)
    for group in range(2):
        cells = join_halves([field_ref[group, r] for r in range(ROWS)])
        for c in range(ROWS):
            plain_ref[pl.ds(8 * group, 8), c, :] = cells[c]
    mine = plain_ref[lax.axis_index("tile")]
    for other in range(out_ref.shape[0]):
        out_ref[other] = mine


def transport(src, flip, gathered, target, speed, rows, copies):
    return pl.pallas_call(
        transport_kernel,
        out_shape=shape(copies, ROWS, 128),
        in_specs=[SMEM] + [VMEM] * 5,
        out_specs=VMEM,
        scratch_shapes=[
            pltpu.VMEM((2, ROWS, 8, 128), f32),
            pltpu.VMEM((4 * TILES, 128), f32),
            pltpu.VMEM((4 * TILES, 128), f32),
            pltpu.VMEM((TILES, ROWS, 128), f32),
            pltpu.VMEM((2, ROWS, 8, 128), f32),
        ],
        compiler_params=GRANT,
        name="transport",
    )(src, flip, gathered, target, speed, rows)


def exchange(values, axis):
    return lax.all_to_all(values, axis, split_axis=0, concat_axis=0, tiled=True)


def to_lines(fields):
    lead = fields.shape[:-2]
    fields = fields.reshape(*lead, L, ROWS, 128)
    return jnp.swapaxes(fields, -3, -2).reshape(*lead, FIELD, 128)


def from_lines(lines):
    lead = lines.shape[:-2]
    lines = lines.reshape(*lead, ROWS, L, 128)
    return jnp.swapaxes(lines, -3, -2).reshape(*lead, L, ROWS * 128)


def body(
    control,
    perturbations,
    diffusivity,
    flow,
    observed,
    obs_weight,
    neighbour_tile,
    neighbour_edge,
    departure,
):
    source = (neighbour_edge * TILES + neighbour_tile).reshape(-1)
    flips = (departure[:, :, 0] != 0).astype(jnp.int32) * S

    def by_lane(values):
        return jnp.repeat(values.T.reshape(2, 2 * TILES), L, axis=1)

    place = (neighbour_edge % 2) * S + neighbour_tile * L
    index = by_lane(place) + jnp.arange(128, dtype=jnp.int32) % L
    table = jnp.stack([index, by_lane(neighbour_edge // 2), by_lane(flips)], axis=1).reshape(6, 128)
    flip = flips.T.reshape(4 * TILES, 1)
    control_lines = to_lines(control[:, 0])

    packed, rows = pack_first(
        control_lines,
        flow[:, 0],
        diffusivity.reshape(ROWS, 128),
        to_lines(obs_weight[0]),
        to_lines(observed[0]),
    )
    own_rate = spread_rate(rows)
    received = exchange(packed, "tile")
    series, rate, goal, speed = frame_forward(table, received)
    smoothed = tile_smooth(False, control_lines, exchange(series, "tile"), own_rate)

    spread = to_lines(perturbations[:, 0])
    increment = jnp.sum(exchange(increments(spread, smoothed), "member"), axis=0)
    gathered = exchange(jnp.broadcast_to(increment[None], (TILES, ROWS, 128)), "tile")
    sensitivity = transport(source, flip, gathered, goal, speed, rows, V * L)
    sensitivity = exchange(sensitivity, "member")
    projected, frames = project(spread, sensitivity)
    series = frame_adjoint(table, exchange(frames, "tile"), rate)
    mixed = tile_smooth(True, projected, exchange(series, "tile"), own_rate, control_lines)
    return from_lines(mixed)[:, None]


def solution(mesh):
    in_specs = (
        P("member", "tile", None, None),
        P("member", "tile", None, None, None),
        P("tile", None),
        P(None, "tile", None, None),
        P("tile", None, None, None),
        P("tile", None, None, None),
        P(),
        P(),
        P(),
    )
    out_specs = P("member", "tile", None, None)
    return jax.shard_map(body, mesh=mesh, in_specs=in_specs, out_specs=out_specs, check_vma=False)
```
